128 devices in a mesh: pix: 8 (over z, y_lo), mem: 16 (over y_hi, x, core).
Axes of the slice: x: 4, y: 4 (y_hi: 2, y_lo: 2; y = y_hi * 2 + y_lo), z: 4, core: 2. Of those that a mesh axis runs over, the one named last changes fastest.
Arguments:
- alpha: bfloat16 [16, 1024, 32, 128], P('mem', 'pix'), may hold values from -6 to 6
- perturbations: bfloat16 [16, 1024, 32, 128], P('mem', 'pix'), may hold values from -6 to 6
- loc_weights: bfloat16 [1024, 9, 128, 128], P('pix'), may hold values from -0.1875 to 0.1875
- static_ctl: float32 [1024, 32, 128], P('pix'), may hold values from -6 to 6
- static_sd: bfloat16 [1024, 32, 128], P('pix'), may hold values from 0.5 to 2
- innovation: float32 [1024, 32, 128], P('pix'), may hold values from -6 to 6
- obs_weight: bfloat16 [1024, 32, 128], P('pix'), may hold values from 0.25 to 4
- neighbours: int32 [1024, 9], P('pix'), may hold values from 0 to 255, as said below
- outbound_blocks: int32 [8, 8, 16], replicated, may hold values from 0 to 127, as said below
- send_counts: int32 [8, 8], replicated, may hold values from 0 to 16, as said below
Outputs:
- increment: float32 [1024, 32, 128], P('pix')
- grad_static: float32 [1024, 32, 128], P('pix')
- grad_alpha: float32 [16, 1024, 32, 128], P('mem', 'pix')
The draws below stay inside these ranges and needn't reach their ends.
Inputs may be any that keep to these rules, and one draw needn't show every extreme that they name: neighbours[b, s] for s = 0 is b % 128. An entry below 128 names a block of the same shard; an entry n of 128 or more names halo slot n - 128 = p * 16 + c of that shard, the c-th block that shard p sends to it, and then c < send_counts[p, shard] and p is the shard just below or just above it. outbound_blocks[p, q] holds 16 distinct block numbers local to shard p; the first send_counts[p, q] of them are sent to shard q. send_counts[p, q] is 0 unless q = p - 1 or q = p + 1 (no wrap); those entries lie between 8 and 16, and send_counts[0, 1] equals 16.
All inputs are finite; a program needn't handle non-finite values.
Results may differ from the reference program's by a relative error of at most 0.0022.
Values may be sent and summed in bfloat16 or wider, within the bound.
A program may use at most 192 MiB of HBM per device.

```python
import math
import jax
import jax.numpy as jnp
from jax import lax

CH = 32
BS = 128
NEIGH = 9
NB_DEV = 128
CAP = 16
MEMBERS = 16
NBLK = 1024


def draw_counts(key):
    shards = NBLK // NB_DEV
    counts_table = jax.random.randint(jax.random.fold_in(key, 11), (shards, shards), CAP // 2, CAP + 1)
    row_ids = jnp.arange(shards)[:, None]
    col_ids = jnp.arange(shards)[None, :]
    adjacent = (col_ids == row_ids + 1) | (col_ids == row_ids - 1)
    counts_table = jnp.where((row_ids == 0) & (col_ids == 1), CAP, counts_table)
    counts_table = jnp.where(adjacent, counts_table, 0)
    return counts_table.astype(jnp.int32)


def draw_send_counts(key, part):
    return draw_counts(key)


def draw_outbound_blocks(key, part):
    shards = NBLK // NB_DEV
    scores = jax.random.randint(jax.random.fold_in(key, 21), (shards, shards, NB_DEV), 0, 1 << 20)
    scores = scores * NB_DEV + jnp.arange(NB_DEV, dtype=jnp.int32)
    ordering = jnp.argsort(scores, axis=-1)
    return ordering[:, :, :CAP].astype(jnp.int32)


def draw_neighbours(key, part):
    shards = NBLK // NB_DEV
    counts_table = draw_counts(key)
    span = shards * CAP
    flat_slots = jnp.arange(span, dtype=jnp.int32)
    slot_source = flat_slots // CAP
    slot_rank = flat_slots % CAP

    def one_shard(dest_shard):
        shard_key = jax.random.fold_in(jax.random.fold_in(key, 31), dest_shard)
        draft_table = jax.random.randint(jax.random.fold_in(shard_key, 1), (NB_DEV, NEIGH - 1), 0, NB_DEV)
        shuffle = jax.random.permutation(jax.random.fold_in(shard_key, 2), NB_DEV)
        offset = jax.random.randint(jax.random.fold_in(shard_key, 3), (), 0, NEIGH - 1)
        target_row = shuffle[flat_slots % NB_DEV]
        target_col = (flat_slots // NB_DEV + offset) % (NEIGH - 1)
        usable = (slot_rank < counts_table[slot_source, dest_shard]) & (slot_source != dest_shard)
        values = jnp.where(usable, NB_DEV + flat_slots, draft_table[target_row, target_col])
        draft_table = draft_table.at[target_row, target_col].set(values)
        self_column = jnp.arange(NB_DEV, dtype=jnp.int32)[:, None]
        return jnp.concatenate([self_column, draft_table.astype(jnp.int32)], axis=1)
    whole_table = jax.vmap(one_shard)(jnp.arange(shards, dtype=jnp.int32))
    return whole_table.reshape(NBLK, NEIGH).astype(jnp.int32)


def block_scale(stream_key, extent, cuts, low, largest):
    gain, own = 1.0, jax.random.fold_in(stream_key, 6)
    for position, blocks in cuts:
        draws = jnp.exp(jax.random.uniform(jax.random.fold_in(own, position), (blocks,), jnp.float32, low / len(cuts), largest / len(cuts)))
        gain = gain * jnp.repeat(draws, extent[position] // blocks).reshape([-1 if axis == position else 1 for axis in range(len(extent))])
    return gain


def noise(key, shape, scale, limit, cuts=(), held_as=jnp.bfloat16):
    values = jax.random.normal(key, shape, jnp.float32) * scale
    if len(cuts) > 0:
        values = block_scale(key, shape, cuts, -0.22, 0.18) * values
    return jnp.clip(values, min=-limit, max=limit).astype(held_as)


def setup_inputs(seed: int = 0) -> dict:
    seeds = jax.random.split(jax.random.key(seed), 11)
    return {
        "alpha": noise(seeds[0], (MEMBERS, NBLK, CH, BS), 1.0, 6.0, ((0, 16), (1, 8))),
        "perturbations": noise(seeds[1], (MEMBERS, NBLK, CH, BS), 1.0, 6.0, ((0, 16), (1, 8))),
        "loc_weights": noise(seeds[2], (NBLK, NEIGH, BS, BS), (NEIGH * BS) ** -0.5, 0.1875, ((0, 8),)),
        "static_ctl": noise(seeds[3], (NBLK, CH, BS), 1.0, 6.0, ((0, 8),), jnp.float32),
        "static_sd": jnp.clip(jnp.exp(math.log(2.0) - 1.3862944 * jax.random.uniform(seeds[4], (NBLK, CH, BS), jnp.float32) ** block_scale(seeds[4], (NBLK, CH, BS), ((0, 8),), -0.2, 0.2)), 0.5, 2.0).astype(jnp.bfloat16),
        "innovation": noise(seeds[5], (NBLK, CH, BS), 1.0, 6.0, ((0, 8),), jnp.float32),
        "obs_weight": jnp.clip(jnp.exp(math.log(4.0) - 2.7725887 * jax.random.uniform(seeds[6], (NBLK, CH, BS), jnp.float32) ** block_scale(seeds[6], (NBLK, CH, BS), ((0, 8),), -0.2, 0.2)), 0.25, 4.0).astype(jnp.bfloat16),
        "neighbours": draw_neighbours(jax.random.fold_in(seeds[10], 71), 0),
        "outbound_blocks": draw_outbound_blocks(jax.random.fold_in(seeds[10], 71), 0),
        "send_counts": draw_send_counts(jax.random.fold_in(seeds[10], 71), 0),
    }


def block_map(neighbours, outbound_blocks, send_counts):
    owner = (jnp.arange(NBLK, dtype=jnp.int32) // NB_DEV)[:, None]
    halo_index = jnp.maximum(neighbours - NB_DEV, 0).astype(jnp.int32)
    source = (halo_index // CAP).astype(jnp.int32)
    slot_rank = (halo_index % CAP).astype(jnp.int32)
    is_local = neighbours < NB_DEV
    remote = source * NB_DEV + outbound_blocks[source, owner, slot_rank]
    target = jnp.where(is_local, owner * NB_DEV + neighbours, remote).astype(jnp.int32)
    allowed = slot_rank < send_counts[source, owner]
    keep_mask = jnp.where(is_local | allowed, 1.0, 0.0).astype(jnp.float32)
    return (target, keep_mask)

def reference(alpha, perturbations, loc_weights, static_ctl, static_sd, innovation, obs_weight, neighbours, outbound_blocks, send_counts):
    target, keep_mask = block_map(neighbours, outbound_blocks, send_counts)
    weights_full = loc_weights.astype(jnp.float32)
    spread = 1.0 / math.sqrt(MEMBERS - 1)

    def forward_one(member_pair):
        control, member_index = member_pair
        picked = control.astype(jnp.float32)[target] * keep_mask[:, :, None, None]
        localized = jnp.einsum('bsci,bsij->bcj', picked, weights_full, precision=lax.Precision.HIGHEST)
        return member_index.astype(jnp.float32) * localized
    member_terms = lax.map(forward_one, (alpha, perturbations))
    deviation = static_sd.astype(jnp.float32)
    increment = deviation * static_ctl + lax.optimization_barrier(jnp.sum(member_terms, axis=0)) * spread
    residual = obs_weight.astype(jnp.float32) * (increment - innovation)
    grad_static = static_ctl + deviation * residual
    flat_target = target.reshape(-1)

    def adjoint_one(member_pair):
        control, member_index = member_pair
        rounded = lax.optimization_barrier((member_index.astype(jnp.float32) * residual * spread).astype(jnp.bfloat16))
        focus_field = rounded.astype(jnp.float32)
        pieces = jnp.einsum('bcj,bsij->bsci', focus_field, weights_full, precision=lax.Precision.HIGHEST)
        pieces = pieces * keep_mask[:, :, None, None]
        summed = jax.ops.segment_sum(pieces.reshape(NBLK * NEIGH, CH, BS), flat_target, num_segments=NBLK)
        return control.astype(jnp.float32) + summed
    grad_alpha = lax.map(adjoint_one, (alpha, perturbations))
    return (increment, grad_static, grad_alpha)
```

```python
import functools
import math

import jax
import jax.numpy as jnp
from jax import lax
from jax.experimental import pallas as pl
from jax.experimental.pallas import tpu as pltpu
from jax.sharding import PartitionSpec as P

F32, BF16 = jnp.float32, jnp.bfloat16
MESH = pl.DeviceIdType.MESH
HBM = pl.BlockSpec(memory_space=pl.ANY)
VMEM = pl.BlockSpec(memory_space=pltpu.VMEM)
SMEM = pl.BlockSpec(memory_space=pltpu.SMEM)
LIMIT = 62 * 2**20


def remote(src, dst, send, recv, device):
    return pltpu.make_async_remote_copy(
        src_ref=src, dst_ref=dst, send_sem=send, recv_sem=recv, device_id=device, device_id_type=MESH
    )


def meet(devices):
    barrier = pltpu.get_barrier_semaphore()
    for device in devices:
        pl.semaphore_signal(barrier, inc=1, device_id=device, device_id_type=MESH)
    pl.semaphore_wait(barrier, len(devices))


def places(shards, members):
    pix, mem = lax.axis_index("pix"), lax.axis_index("mem")
    core = lax.rem(mem, 2)
    partner = (pix, mem + 1 - 2 * core)
    below = (lax.rem(pix + shards - 1, shards), mem)
    above = (lax.rem(pix + 1, shards), mem)
    return pix, mem, core, partner, below, above


def forward_kernel(
    dims, table, alpha_h, pert_h, w_h, ens_h, other_pert_h,
    alpha_v, mine, theirs, pert0, pert1, wv, terms, recv, gathered, other, packed,
    w_sem, local_sem, out_sem, pair_send, pair_recv, halo_send, halo_recv, rs_send, rs_recv, ag_send, ag_recv,
):
    shards, members, blocks, neigh, cap = dims
    half, chips = blocks // 2, members // 2
    per = half // chips
    pix, mem, core, partner, below, above = places(shards, members)
    chip = mem // 2

    def w_copy(step):
        k = lax.rem(chip + 1 + step, chips)
        return pltpu.make_async_copy(
            w_h.at[pl.ds(core * half + k * per, per)], wv.at[pl.ds(k * per, per)], w_sem.at[step]
        )

    loads = [
        pltpu.make_async_copy(alpha_h, alpha_v, local_sem.at[0]),
        pltpu.make_async_copy(alpha_h, mine.at[pl.ds(0, blocks)], local_sem.at[1]),
        pltpu.make_async_copy(pert_h.at[pl.ds(core * half, half)], pert0, local_sem.at[2]),
    ]
    for load in loads:
        load.start()
    for step in range(chips):
        w_copy(step).start()
    zero = jnp.zeros(mine.shape[1:], BF16)
    mine[blocks + 2 * cap] = zero
    theirs[blocks + 2 * cap] = zero
    peers = [(pix, 2 * lax.rem(chip + j, chips) + core) for j in range(1, chips)]
    meet([partner, below, above] + peers)
    pair = [
        remote(alpha_h, theirs.at[pl.ds(0, blocks)], pair_send.at[0], pair_recv.at[0], partner),
        remote(pert_h.at[pl.ds((1 - core) * half, half)], pert1, pair_send.at[1], pair_recv.at[1], partner),
        remote(
            mine.at[pl.ds(blocks, 2 * cap)], theirs.at[pl.ds(blocks, 2 * cap)], pair_send.at[2], pair_recv.at[2], partner
        ),
    ]
    loads[0].wait()
    base = half * neigh
    for c in range(2 * cap):
        keep = table[base + 2 * cap + c].astype(F32)
        packed[c] = (alpha_v[table[base + c]].astype(F32) * keep).astype(BF16)
    halo = [
        remote(packed.at[pl.ds(0, cap)], mine.at[pl.ds(blocks + cap, cap)], halo_send.at[0], halo_recv.at[1], below),
        remote(packed.at[pl.ds(cap, cap)], mine.at[pl.ds(blocks, cap)], halo_send.at[1], halo_recv.at[0], above),
    ]
    halo[0].start()
    halo[1].start()
    pair[0].start()
    pair[1].start()
    halo[0].wait_recv()
    halo[1].wait_recv()
    pair[2].start()
    loads[1].wait()
    loads[2].wait()
    for copy in pair:
        copy.wait_recv()

    def rs_copy(k):
        return remote(
            terms.at[pl.ds(k * per, per)], recv.at[chip], rs_send.at[k], rs_recv.at[chip], (pix, 2 * k + core)
        )

    def one_step(step, carry):
        k = lax.rem(chip + 1 + step, chips)
        w_copy(step).wait()
        for j in range(per):
            i = k * per + j
            picked = [table[i * neigh + s] for s in range(neigh)]
            rows = jnp.concatenate(
                [jnp.concatenate([field[n] for n in picked], axis=1) for field in (mine, theirs)], axis=0
            )
            weights = wv[i].reshape(neigh * wv.shape[2], wv.shape[3])
            local = jnp.dot(rows, weights, preferred_element_type=F32)
            ch = local.shape[0] // 2
            terms[i] = pert0[i].astype(F32) * local[:ch] + pert1[i].astype(F32) * local[ch:]

        @pl.when(step < chips - 1)
        def _():
            rs_copy(k).start()

        return carry

    lax.fori_loop(0, chips, one_step, 0)
    other_pert = pltpu.make_async_copy(pert1, other_pert_h, out_sem.at[2])
    other_pert.start()
    for j in range(1, chips):
        src = lax.rem(chip + j, chips)
        remote(terms.at[pl.ds(0, per)], recv.at[src], rs_send.at[src], rs_recv.at[src], partner).wait_recv()
    recv[chip] = terms[pl.ds(chip * per, per)]
    spread = 1.0 / math.sqrt(members - 1)
    for i in range(per):
        total = recv[0, i]
        for k in range(1, chips):
            total = total + recv[k, i]
        gathered[chip, i] = total * spread
    sends = [
        remote(gathered.at[chip], gathered.at[chip], ag_send.at[j - 1], ag_recv.at[chip], peers[j - 1])
        for j in range(1, chips)
    ]
    for copy in sends:
        copy.start()
    for j in range(1, chips):
        src = lax.rem(chip + j, chips)
        remote(gathered.at[src], gathered.at[src], ag_send.at[j - 1], ag_recv.at[src], partner).wait_recv()
    swap = remote(gathered, other, pair_send.at[3], pair_recv.at[3], partner)
    swap.start()
    outs = [
        pltpu.make_async_copy(gathered, ens_h.at[pl.ds(core * chips, chips)], out_sem.at[0]),
        pltpu.make_async_copy(other, ens_h.at[pl.ds((1 - core) * chips, chips)], out_sem.at[1]),
    ]
    outs[0].start()
    swap.wait_recv()
    outs[1].start()
    for copy in halo + pair + [swap] + sends:
        copy.wait_send()
    for j in range(1, chips):
        rs_copy(lax.rem(chip + j, chips)).wait_send()
    for copy in outs + [other_pert]:
        copy.wait()


def adjoint_kernel(
    dims, table, where, ens_h, ctl_h, dev_h, inn_h, wgt_h, pert_h, other_pert_h, w_h, inc_h, gs_h, acc_out, send_out,
    ens, ctl, dev, inn, wgt, pert0, pert1, wv, inc, gs, acc0, acc1, w_sem, in_sem, out_sem,
):
    shards, members, blocks, neigh, cap = dims
    half = blocks // 2
    chunks = w_sem.shape[0]
    per = half // chunks
    core = where[0]
    spread = 1.0 / math.sqrt(members - 1)
    starts = (core * half, (1 - core) * half)
    loads = [
        [
            pltpu.make_async_copy(src.at[pl.ds(starts[h], half)], dst.at[h], in_sem.at[h, n])
            for n, (src, dst) in enumerate(
                ((ens_h, ens), (ctl_h, ctl), (dev_h, dev), (inn_h, inn), (wgt_h, wgt))
            )
        ]
        for h in range(2)
    ]
    loads[0] += [
        pltpu.make_async_copy(pert_h.at[pl.ds(core * half, half)], pert0, in_sem.at[0, 5]),
        pltpu.make_async_copy(other_pert_h, pert1, in_sem.at[0, 6]),
    ]

    def w_copy(j):
        return pltpu.make_async_copy(
            w_h.at[pl.ds(core * half + j * per, per)], wv.at[pl.ds(j * per, per)], w_sem.at[j]
        )

    for load in loads[0]:
        load.start()
    for j in range(chunks):
        w_copy(j).start()
    for load in loads[1]:
        load.start()
    acc0[...] = jnp.zeros_like(acc0)
    acc1[...] = jnp.zeros_like(acc1)

    def fields(h, i):
        scale = dev[h, i].astype(F32)
        increment = scale * ctl[h, i] + ens[h, i].astype(F32)
        residual = wgt[h, i].astype(F32) * (increment - inn[h, i])
        inc[h, i] = increment
        gs[h, i] = ctl[h, i] + scale * residual
        return residual

    for load in loads[0]:
        load.wait()

    def one_chunk(j, carry):
        w_copy(j).wait()
        for jj in range(per):
            i = j * per + jj
            residual = fields(0, i)
            focus = jnp.concatenate(
                [(p[i].astype(F32) * residual * spread).astype(BF16) for p in (pert0, pert1)], axis=0
            )
            weights = wv[i].reshape(neigh * wv.shape[2], wv.shape[3])
            pieces = lax.dot_general(
                focus, weights, (((1,), (1,)), ((), ())), preferred_element_type=F32
            )
            ch, width = focus.shape[0] // 2, wv.shape[2]
            for s in range(neigh):
                n = table[i * neigh + s]
                acc0[n] += pieces[:ch, s * width : (s + 1) * width]
                acc1[n] += pieces[ch:, s * width : (s + 1) * width]
        return carry

    lax.fori_loop(0, chunks, one_chunk, 0)
    for load in loads[1]:
        load.wait()
    stores = [
        [
            pltpu.make_async_copy(src.at[h], dst.at[pl.ds(starts[h], half)], out_sem.at[h, n])
            for n, (src, dst) in enumerate(((inc, inc_h), (gs, gs_h)))
        ]
        for h in range(2)
    ]
    for store in stores[0]:
        store.start()

    def other_half(i, carry):
        fields(1, i)
        return carry

    lax.fori_loop(0, half, other_half, 0, unroll=4)
    for store in stores[1]:
        store.start()
    last = pltpu.make_async_copy(acc0, acc_out, out_sem.at[0, 2])
    last.start()
    send_out[...] = acc1[pl.ds(0, blocks + 2 * cap)].astype(send_out.dtype)
    last.wait()
    for h in range(2):
        for store in stores[h]:
            store.wait()


def return_kernel(
    dims, acc_h, send_ref, partner_ref, back_ref, half_buf, back_buf, own_rim, rim, packed,
    in_sem, pair_send, pair_recv, halo_send, halo_recv,
):
    shards, members, blocks, neigh, cap = dims
    pix, mem, core, partner, below, above = places(shards, members)
    load = pltpu.make_async_copy(acc_h.at[pl.ds(blocks, 2 * cap)], own_rim, in_sem)
    load.start()
    meet([partner, below, above])
    pair = [
        remote(send_ref.at[pl.ds(blocks, 2 * cap)], rim, pair_send.at[0], pair_recv.at[0], partner),
        remote(send_ref.at[pl.ds(0, blocks)], half_buf, pair_send.at[1], pair_recv.at[1], partner),
    ]
    pair[0].start()
    pair[1].start()
    load.wait()
    pair[0].wait_recv()
    packed[...] = (own_rim[...] + rim[...].astype(F32)).astype(BF16)
    halo = [
        remote(packed.at[pl.ds(0, cap)], back_buf.at[pl.ds(cap, cap)], halo_send.at[0], halo_recv.at[1], below),
        remote(packed.at[pl.ds(cap, cap)], back_buf.at[pl.ds(0, cap)], halo_send.at[1], halo_recv.at[0], above),
    ]
    halo[0].start()
    halo[1].start()
    pair[1].wait_recv()
    partner_ref[...] = half_buf[...]
    halo[0].wait_recv()
    halo[1].wait_recv()
    back_ref[...] = back_buf[...]
    for copy in pair + halo:
        copy.wait_send()


def finish_kernel(dims, table, alpha_ref, acc_ref, partner_ref, back_ref, out_ref):
    shards, members, blocks, neigh, cap = dims
    base = (blocks // 2) * neigh

    def one(i, carry):
        out_ref[i] = alpha_ref[i].astype(F32) + acc_ref[i] + partner_ref[i].astype(F32)
        return carry

    lax.fori_loop(0, blocks, one, 0, unroll=8)
    for c in range(2 * cap):
        out_ref[table[base + c]] += back_ref[c].astype(F32) * table[base + 2 * cap + c].astype(F32)


def per_device(
    alpha, perturbations, loc_weights, static_ctl, static_sd, innovation, obs_weight, neighbours, outbound_blocks,
    send_counts,
):
    shards, members = lax.axis_size("pix"), lax.axis_size("mem")
    me = lax.axis_index("pix")
    core = lax.axis_index("mem") % 2
    alpha, pert = alpha[0], perturbations[0]
    blocks, ch, width = alpha.shape
    neigh, cap = neighbours.shape[1], outbound_blocks.shape[2]
    half, chips = blocks // 2, members // 2
    per, ext = half // chips, blocks + 2 * cap + 1
    dims = (shards, members, blocks, neigh, cap)

    mine = lax.dynamic_slice_in_dim(neighbours, core * half, half, 0)
    slot = mine - blocks
    source = slot // cap
    rim_slot = jnp.where(
        source == me - 1, slot - (me - 1) * cap, jnp.where(source == me + 1, slot - me * cap, 2 * cap)
    )
    targets = jnp.where(mine < blocks, mine, blocks + rim_slot).reshape(half * neigh)
    below, above = (me + shards - 1) % shards, (me + 1) % shards
    rows = jnp.concatenate([outbound_blocks[me, below], outbound_blocks[me, above]])
    rank = jnp.arange(cap, dtype=jnp.int32)
    keep = jnp.concatenate([rank < send_counts[me, below], rank < send_counts[me, above]]).astype(jnp.int32)
    table = jnp.concatenate([targets, rows, keep]).astype(jnp.int32)

    tile = (ch, width)
    dma = pltpu.SemaphoreType.DMA
    ens, other_pert = pl.pallas_call(
        functools.partial(forward_kernel, dims),
        out_shape=(
            jax.ShapeDtypeStruct((members, per, *tile), F32),
            jax.ShapeDtypeStruct((half, *tile), BF16),
        ),
        in_specs=[SMEM, HBM, HBM, HBM],
        out_specs=(HBM, HBM),
        scratch_shapes=[
            pltpu.VMEM((blocks, *tile), BF16),
            pltpu.VMEM((ext, *tile), BF16),
            pltpu.VMEM((ext, *tile), BF16),
            pltpu.VMEM((half, *tile), BF16),
            pltpu.VMEM((half, *tile), BF16),
            pltpu.VMEM((half, neigh, width, width), BF16),
            pltpu.VMEM((half, *tile), F32),
            pltpu.VMEM((chips, per, *tile), F32),
            pltpu.VMEM((chips, per, *tile), F32),
            pltpu.VMEM((chips, per, *tile), F32),
            pltpu.VMEM((2 * cap, *tile), BF16),
            dma((chips,)), dma((3,)), dma((3,)), dma((4,)), dma((4,)), dma((2,)), dma((2,)),
            dma((chips,)), dma((chips,)), dma((chips,)), dma((chips,)),
        ],
        compiler_params=pltpu.CompilerParams(collective_id=0, has_side_effects=True, vmem_limit_bytes=LIMIT),
        name="forward",
    )(table, alpha, pert, loc_weights)

    chunks = max(half // 8, 1)
    increment, grad_static, acc, sending = pl.pallas_call(
        functools.partial(adjoint_kernel, dims),
        out_shape=(
            jax.ShapeDtypeStruct((blocks, *tile), F32),
            jax.ShapeDtypeStruct((blocks, *tile), F32),
            jax.ShapeDtypeStruct((ext, *tile), F32),
            jax.ShapeDtypeStruct((ext - 1, *tile), BF16),
        ),
        in_specs=[SMEM, SMEM] + [HBM] * 8,
        out_specs=(HBM, HBM, HBM, VMEM),
        scratch_shapes=[
            pltpu.VMEM((2, half, *tile), F32),
            pltpu.VMEM((2, half, *tile), F32),
            pltpu.VMEM((2, half, *tile), BF16),
            pltpu.VMEM((2, half, *tile), F32),
            pltpu.VMEM((2, half, *tile), BF16),
            pltpu.VMEM((half, *tile), BF16),
            pltpu.VMEM((half, *tile), BF16),
            pltpu.VMEM((half, neigh, width, width), BF16),
            pltpu.VMEM((2, half, *tile), F32),
            pltpu.VMEM((2, half, *tile), F32),
            pltpu.VMEM((ext, *tile), F32),
            pltpu.VMEM((ext, *tile), F32),
            dma((chunks,)), dma((2, 7)), dma((2, 3)),
        ],
        compiler_params=pltpu.CompilerParams(vmem_limit_bytes=LIMIT),
        name="adjoint",
    )(
        table, core.reshape(1), ens.reshape(blocks, *tile), static_ctl, static_sd, innovation, obs_weight, pert,
        other_pert, loc_weights,
    )

    from_partner, came_back = pl.pallas_call(
        functools.partial(return_kernel, dims),
        out_shape=(
            jax.ShapeDtypeStruct((blocks, *tile), BF16),
            jax.ShapeDtypeStruct((2 * cap, *tile), BF16),
        ),
        in_specs=[HBM, VMEM],
        out_specs=(VMEM, VMEM),
        scratch_shapes=[
            pltpu.VMEM((blocks, *tile), BF16),
            pltpu.VMEM((2 * cap, *tile), BF16),
            pltpu.VMEM((2 * cap, *tile), F32),
            pltpu.VMEM((2 * cap, *tile), BF16),
            pltpu.VMEM((2 * cap, *tile), BF16),
            dma, dma((2,)), dma((2,)), dma((2,)), dma((2,)),
        ],
        compiler_params=pltpu.CompilerParams(collective_id=1, has_side_effects=True, vmem_limit_bytes=LIMIT),
        name="returns",
    )(acc, sending)

    grad_alpha = pl.pallas_call(
        functools.partial(finish_kernel, dims),
        out_shape=jax.ShapeDtypeStruct((blocks, *tile), F32),
        in_specs=[SMEM, VMEM, VMEM, VMEM, VMEM],
        out_specs=VMEM,
        compiler_params=pltpu.CompilerParams(vmem_limit_bytes=LIMIT),
        name="finish",
    )(table, alpha, acc, from_partner, came_back)
    return increment, grad_static, grad_alpha[None]


def solution(mesh):
    placed = (
        P("mem", "pix", None, None),
        P("mem", "pix", None, None),
        P("pix", None, None, None),
        P("pix", None, None),
        P("pix", None, None),
        P("pix", None, None),
        P("pix", None, None),
        P("pix", None),
        P(),
        P(),
    )
    return jax.shard_map(
        per_device,
        mesh=mesh,
        in_specs=placed,
        out_specs=(P("pix", None, None), P("pix", None, None), P("mem", "pix", None, None)),
        check_vma=False,
    )
```

```python
import functools
import math

import jax
import jax.numpy as jnp
from jax import lax
from jax.experimental import pallas as pl
from jax.experimental.pallas import tpu as pltpu
from jax.sharding import PartitionSpec as P

F32, BF16 = jnp.float32, jnp.bfloat16
MESH = pl.DeviceIdType.MESH
HBM = pl.BlockSpec(memory_space=pl.ANY)
VMEM = pl.BlockSpec(memory_space=pltpu.VMEM)
SMEM = pl.BlockSpec(memory_space=pltpu.SMEM)
LIMIT = 62 * 2**20


def remote(src, dst, send, recv, device):
    return pltpu.make_async_remote_copy(
        src_ref=src, dst_ref=dst, send_sem=send, recv_sem=recv, device_id=device, device_id_type=MESH
    )


def meet(devices):
    barrier = pltpu.get_barrier_semaphore()
    for device in devices:
        pl.semaphore_signal(barrier, inc=1, device_id=device, device_id_type=MESH)
    pl.semaphore_wait(barrier, len(devices))


def places(shards, members):
    pix, mem = lax.axis_index("pix"), lax.axis_index("mem")
    core = lax.rem(mem, 2)
    partner = (pix, mem + 1 - 2 * core)
    below = (lax.rem(pix + shards - 1, shards), mem)
    above = (lax.rem(pix + 1, shards), mem)
    return pix, mem, core, partner, below, above


def slot_of(names, row, s, pix, blocks, cap):
    n = names[row, s]
    rim = n - cap * (pix - 1) - jnp.where(n >= blocks + cap * pix, cap, 0)
    return jnp.where(n < blocks, n, rim)


def rim_block(outbound, counts, pix, shards, c, cap):
    side = lax.rem(pix + (shards - 1 if c < cap else 1), shards)
    rank = c % cap
    return outbound[pix, side, rank], jnp.where(rank < counts[pix, side], 1.0, 0.0).astype(F32)


def forward_kernel(
    dims, names, outbound, counts, alpha_h, pert_h, w_h, ens_h, other_pert_h,
    alpha_v, mine, theirs, pert0, pert1, wv, terms, recv, gathered, other, packed,
    w_sem, local_sem, out_sem, pair_send, pair_recv, halo_send, halo_recv, rs_send, rs_recv, ag_send, ag_recv, swap_send, swap_recv,
):
    shards, members, blocks, neigh, cap = dims
    half, chips = blocks // 2, members // 2
    per = half // chips
    pix, mem, core, partner, below, above = places(shards, members)
    chip = mem // 2

    def w_copy(step):
        k = lax.rem(chip + 1 + step, chips)
        return pltpu.make_async_copy(
            w_h.at[pl.ds(core * half + k * per, per)], wv.at[pl.ds(k * per, per)], w_sem.at[step]
        )

    loads = [
        pltpu.make_async_copy(alpha_h, alpha_v, local_sem.at[0]),
        pltpu.make_async_copy(alpha_h, mine.at[pl.ds(0, blocks)], local_sem.at[1]),
        pltpu.make_async_copy(pert_h.at[pl.ds(core * half, half)], pert0, local_sem.at[2]),
    ]
    for load in loads:
        load.start()
    for step in range(chips):
        w_copy(step).start()
    peers = [(pix, 2 * lax.rem(chip + j, chips) + core) for j in range(1, chips)]
    meet([partner, below, above] + peers)
    pair = [
        remote(alpha_h, theirs.at[pl.ds(0, blocks)], pair_send.at[0], pair_recv.at[0], partner),
        remote(pert_h.at[pl.ds((1 - core) * half, half)], pert1, pair_send.at[1], pair_recv.at[1], partner),
        remote(
            mine.at[pl.ds(blocks, 2 * cap)], theirs.at[pl.ds(blocks, 2 * cap)], pair_send.at[2], pair_recv.at[2], partner
        ),
    ]
    loads[0].wait()
    for c in range(2 * cap):
        row, keep = rim_block(outbound, counts, pix, shards, c, cap)
        packed[c] = (alpha_v[row].astype(F32) * keep).astype(BF16)
    halo = [
        remote(packed.at[pl.ds(0, cap)], mine.at[pl.ds(blocks + cap, cap)], halo_send.at[0], halo_recv.at[1], below),
        remote(packed.at[pl.ds(cap, cap)], mine.at[pl.ds(blocks, cap)], halo_send.at[1], halo_recv.at[0], above),
    ]
    halo[0].start()
    halo[1].start()
    pair[0].start()
    pair[1].start()
    halo[0].wait_recv()
    halo[1].wait_recv()
    pair[2].start()
    loads[1].wait()
    loads[2].wait()
    for copy in pair:
        copy.wait_recv()

    def rs_copy(k):
        return remote(
            terms.at[pl.ds(k * per, per)], recv.at[chip], rs_send.at[k], rs_recv.at[chip], (pix, 2 * k + core)
        )

    def one_step(step, carry):
        k = lax.rem(chip + 1 + step, chips)
        w_copy(step).wait()
        for j in range(per):
            i = k * per + j
            picked = [slot_of(names, core * half + i, s, pix, blocks, cap) for s in range(neigh)]
            rows = jnp.concatenate(
                [jnp.concatenate([field[n] for n in picked], axis=1) for field in (mine, theirs)], axis=0
            )
            weights = wv[i].reshape(neigh * wv.shape[2], wv.shape[3])
            local = jnp.dot(rows, weights, preferred_element_type=F32)
            ch = local.shape[0] // 2
            terms[i] = (pert0[i].astype(F32) * local[:ch] + pert1[i].astype(F32) * local[ch:]).astype(BF16)

        @pl.when(step < chips - 1)
        def _():
            rs_copy(k).start()

        return carry

    lax.fori_loop(0, chips, one_step, 0)
    other_pert = pltpu.make_async_copy(pert1, other_pert_h, out_sem.at[2])
    other_pert.start()
    for j in range(1, chips):
        src = lax.rem(chip + j, chips)
        remote(terms.at[pl.ds(0, per)], recv.at[src], rs_send.at[src], rs_recv.at[src], partner).wait_recv()
    recv[chip] = terms[pl.ds(chip * per, per)]
    spread = 1.0 / math.sqrt(members - 1)
    for i in range(per):
        total = recv[0, i].astype(F32)
        for k in range(1, chips):
            total = total + recv[k, i].astype(F32)
        gathered[chip, i] = (total * spread).astype(BF16)
    sends = [
        remote(gathered.at[chip], gathered.at[chip], ag_send.at[j - 1], ag_recv.at[chip], peers[j - 1])
        for j in range(1, chips)
    ]
    for copy in sends:
        copy.start()

    def swap_copy(k, j):
        return remote(gathered.at[k], other.at[k], swap_send.at[j], swap_recv.at[k], partner)

    swaps = [swap_copy(chip, 0)]
    swaps[0].start()
    for j in range(1, chips):
        src = lax.rem(chip + j, chips)
        remote(gathered.at[src], gathered.at[src], ag_send.at[j - 1], ag_recv.at[src], partner).wait_recv()
        swaps.append(swap_copy(src, j))
        swaps[j].start()
    outs = [
        pltpu.make_async_copy(gathered, ens_h.at[pl.ds(core * chips, chips)], out_sem.at[0]),
        pltpu.make_async_copy(other, ens_h.at[pl.ds((1 - core) * chips, chips)], out_sem.at[1]),
    ]
    outs[0].start()
    for copy in swaps:
        copy.wait_recv()
    outs[1].start()
    for copy in halo + pair + swaps + sends:
        copy.wait_send()
    for j in range(1, chips):
        rs_copy(lax.rem(chip + j, chips)).wait_send()
    for copy in outs + [other_pert]:
        copy.wait()


def adjoint_kernel(
    dims, names, ens_h, ctl_h, dev_h, inn_h, wgt_h, pert_h, other_pert_h, w_h, inc_h, gs_h, acc_out, send_out,
    ens, ctl, dev, inn, wgt, pert0, pert1, wv, inc, gs, acc0, acc1, w_sem, in_sem, out_sem,
):
    shards, members, blocks, neigh, cap = dims
    half = blocks // 2
    chunks = w_sem.shape[0]
    per = half // chunks
    pix, core = lax.axis_index("pix"), lax.rem(lax.axis_index("mem"), 2)
    spread = 1.0 / math.sqrt(members - 1)
    starts = (core * half, (1 - core) * half)
    loads = [
        [
            pltpu.make_async_copy(src.at[pl.ds(starts[h], half)], dst.at[h], in_sem.at[h, n])
            for n, (src, dst) in enumerate(
                ((ens_h, ens), (ctl_h, ctl), (dev_h, dev), (inn_h, inn), (wgt_h, wgt))
            )
        ]
        for h in range(2)
    ]
    loads[0] += [
        pltpu.make_async_copy(pert_h.at[pl.ds(core * half, half)], pert0, in_sem.at[0, 5]),
        pltpu.make_async_copy(other_pert_h, pert1, in_sem.at[0, 6]),
    ]

    def w_copy(j):
        return pltpu.make_async_copy(
            w_h.at[pl.ds(core * half + j * per, per)], wv.at[pl.ds(j * per, per)], w_sem.at[j]
        )

    for load in loads[0]:
        load.start()
    for j in range(chunks):
        w_copy(j).start()
    for load in loads[1]:
        load.start()
    acc0[...] = jnp.zeros_like(acc0)
    acc1[...] = jnp.zeros_like(acc1)

    def fields(h, i):
        scale = dev[h, i].astype(F32)
        increment = scale * ctl[h, i] + ens[h, i].astype(F32)
        residual = wgt[h, i].astype(F32) * (increment - inn[h, i])
        inc[h, i] = increment
        gs[h, i] = ctl[h, i] + scale * residual
        return residual

    for load in loads[0]:
        load.wait()

    def one_chunk(j, carry):
        w_copy(j).wait()
        for jj in range(per):
            i = j * per + jj
            residual = fields(0, i)
            focus = jnp.concatenate(
                [(p[i].astype(F32) * residual * spread).astype(BF16) for p in (pert0, pert1)], axis=0
            )
            weights = wv[i].reshape(neigh * wv.shape[2], wv.shape[3])
            pieces = lax.dot_general(
                focus, weights, (((1,), (1,)), ((), ())), preferred_element_type=F32
            )
            ch, width = focus.shape[0] // 2, wv.shape[2]
            for s in range(neigh):
                n = slot_of(names, core * half + i, s, pix, blocks, cap)
                acc0[n] += pieces[:ch, s * width : (s + 1) * width]
                acc1[n] += pieces[ch:, s * width : (s + 1) * width]
        return carry

    lax.fori_loop(0, chunks, one_chunk, 0)
    for load in loads[1]:
        load.wait()
    stores = [
        [
            pltpu.make_async_copy(src.at[h], dst.at[pl.ds(starts[h], half)], out_sem.at[h, n])
            for n, (src, dst) in enumerate(((inc, inc_h), (gs, gs_h)))
        ]
        for h in range(2)
    ]
    for store in stores[0]:
        store.start()

    def other_half(i, carry):
        fields(1, i)
        return carry

    lax.fori_loop(0, half, other_half, 0, unroll=4)
    for store in stores[1]:
        store.start()
    last = pltpu.make_async_copy(acc0, acc_out, out_sem.at[0, 2])
    last.start()
    send_out[...] = acc1[...].astype(send_out.dtype)
    last.wait()
    for h in range(2):
        for store in stores[h]:
            store.wait()


def return_kernel(
    dims, acc_h, send_ref, partner_ref, back_ref, half_buf, back_buf, own_rim, rim, packed,
    in_sem, pair_send, pair_recv, halo_send, halo_recv,
):
    shards, members, blocks, neigh, cap = dims
    pix, mem, core, partner, below, above = places(shards, members)
    load = pltpu.make_async_copy(acc_h.at[pl.ds(blocks, 2 * cap)], own_rim, in_sem)
    load.start()
    meet([partner, below, above])
    pair = [
        remote(send_ref.at[pl.ds(blocks, 2 * cap)], rim, pair_send.at[0], pair_recv.at[0], partner),
        remote(send_ref.at[pl.ds(0, blocks)], half_buf, pair_send.at[1], pair_recv.at[1], partner),
    ]
    pair[0].start()
    pair[1].start()
    load.wait()
    pair[0].wait_recv()
    packed[...] = (own_rim[...] + rim[...].astype(F32)).astype(BF16)
    halo = [
        remote(packed.at[pl.ds(0, cap)], back_buf.at[pl.ds(cap, cap)], halo_send.at[0], halo_recv.at[1], below),
        remote(packed.at[pl.ds(cap, cap)], back_buf.at[pl.ds(0, cap)], halo_send.at[1], halo_recv.at[0], above),
    ]
    halo[0].start()
    halo[1].start()
    pair[1].wait_recv()
    partner_ref[...] = half_buf[...]
    halo[0].wait_recv()
    halo[1].wait_recv()
    back_ref[...] = back_buf[...]
    for copy in pair + halo:
        copy.wait_send()


def finish_kernel(dims, outbound, counts, alpha_ref, acc_ref, partner_ref, back_ref, out_ref):
    shards, members, blocks, neigh, cap = dims
    pix = lax.axis_index("pix")

    def one(i, carry):
        out_ref[i] = alpha_ref[i].astype(F32) + acc_ref[i] + partner_ref[i].astype(F32)
        return carry

    lax.fori_loop(0, blocks, one, 0, unroll=8)
    for c in range(2 * cap):
        row, keep = rim_block(outbound, counts, pix, shards, c, cap)
        out_ref[row] += back_ref[c].astype(F32) * keep


def per_device(
    alpha, perturbations, loc_weights, static_ctl, static_sd, innovation, obs_weight, neighbours, outbound_blocks,
    send_counts,
):
    shards, members = lax.axis_size("pix"), lax.axis_size("mem")
    alpha, pert = alpha[0], perturbations[0]
    blocks, ch, width = alpha.shape
    neigh, cap = neighbours.shape[1], outbound_blocks.shape[2]
    half, chips = blocks // 2, members // 2
    per, ext = half // chips, blocks + 2 * cap
    dims = (shards, members, blocks, neigh, cap)

    tile = (ch, width)
    dma = pltpu.SemaphoreType.DMA
    ens, other_pert = pl.pallas_call(
        functools.partial(forward_kernel, dims),
        out_shape=(
            jax.ShapeDtypeStruct((members, per, *tile), BF16),
            jax.ShapeDtypeStruct((half, *tile), BF16),
        ),
        in_specs=[SMEM, SMEM, SMEM, HBM, HBM, HBM],
        out_specs=(HBM, HBM),
        scratch_shapes=[
            pltpu.VMEM((blocks, *tile), BF16),
            pltpu.VMEM((ext, *tile), BF16),
            pltpu.VMEM((ext, *tile), BF16),
            pltpu.VMEM((half, *tile), BF16),
            pltpu.VMEM((half, *tile), BF16),
            pltpu.VMEM((half, neigh, width, width), BF16),
            pltpu.VMEM((half, *tile), BF16),
            pltpu.VMEM((chips, per, *tile), BF16),
            pltpu.VMEM((chips, per, *tile), BF16),
            pltpu.VMEM((chips, per, *tile), BF16),
            pltpu.VMEM((2 * cap, *tile), BF16),
            dma((chips,)), dma((3,)), dma((3,)), dma((3,)), dma((3,)), dma((2,)), dma((2,)),
            dma((chips,)), dma((chips,)), dma((chips,)), dma((chips,)), dma((chips,)), dma((chips,)),
        ],
        compiler_params=pltpu.CompilerParams(collective_id=0, has_side_effects=True, vmem_limit_bytes=LIMIT),
        name="forward",
    )(neighbours, outbound_blocks, send_counts, alpha, pert, loc_weights)

    chunks = max(half // 8, 1)
    increment, grad_static, acc, sending = pl.pallas_call(
        functools.partial(adjoint_kernel, dims),
        out_shape=(
            jax.ShapeDtypeStruct((blocks, *tile), F32),
            jax.ShapeDtypeStruct((blocks, *tile), F32),
            jax.ShapeDtypeStruct((ext, *tile), F32),
            jax.ShapeDtypeStruct((ext, *tile), BF16),
        ),
        in_specs=[SMEM] + [HBM] * 8,
        out_specs=(HBM, HBM, HBM, VMEM),
        scratch_shapes=[
            pltpu.VMEM((2, half, *tile), BF16),
            pltpu.VMEM((2, half, *tile), F32),
            pltpu.VMEM((2, half, *tile), BF16),
            pltpu.VMEM((2, half, *tile), F32),
            pltpu.VMEM((2, half, *tile), BF16),
            pltpu.VMEM((half, *tile), BF16),
            pltpu.VMEM((half, *tile), BF16),
            pltpu.VMEM((half, neigh, width, width), BF16),
            pltpu.VMEM((2, half, *tile), F32),
            pltpu.VMEM((2, half, *tile), F32),
            pltpu.VMEM((ext, *tile), F32),
            pltpu.VMEM((ext, *tile), F32),
            dma((chunks,)), dma((2, 7)), dma((2, 3)),
        ],
        compiler_params=pltpu.CompilerParams(vmem_limit_bytes=LIMIT),
        name="adjoint",
    )(
        neighbours, ens.reshape(blocks, *tile), static_ctl, static_sd, innovation, obs_weight, pert,
        other_pert, loc_weights,
    )

    from_partner, came_back = pl.pallas_call(
        functools.partial(return_kernel, dims),
        out_shape=(
            jax.ShapeDtypeStruct((blocks, *tile), BF16),
            jax.ShapeDtypeStruct((2 * cap, *tile), BF16),
        ),
        in_specs=[HBM, VMEM],
        out_specs=(VMEM, VMEM),
        scratch_shapes=[
            pltpu.VMEM((blocks, *tile), BF16),
            pltpu.VMEM((2 * cap, *tile), BF16),
            pltpu.VMEM((2 * cap, *tile), F32),
            pltpu.VMEM((2 * cap, *tile), BF16),
            pltpu.VMEM((2 * cap, *tile), BF16),
            dma, dma((2,)), dma((2,)), dma((2,)), dma((2,)),
        ],
        compiler_params=pltpu.CompilerParams(collective_id=1, has_side_effects=True, vmem_limit_bytes=LIMIT),
        name="returns",
    )(acc, sending)

    grad_alpha = pl.pallas_call(
        functools.partial(finish_kernel, dims),
        out_shape=jax.ShapeDtypeStruct((blocks, *tile), F32),
        in_specs=[SMEM, SMEM, VMEM, VMEM, VMEM, VMEM],
        out_specs=VMEM,
        compiler_params=pltpu.CompilerParams(vmem_limit_bytes=LIMIT),
        name="finish",
    )(outbound_blocks, send_counts, alpha, acc, from_partner, came_back)
    return increment, grad_static, grad_alpha[None]


def solution(mesh):
    placed = (
        P("mem", "pix", None, None),
        P("mem", "pix", None, None),
        P("pix", None, None, None),
        P("pix", None, None),
        P("pix", None, None),
        P("pix", None, None),
        P("pix", None, None),
        P("pix", None),
        P(),
        P(),
    )
    return jax.shard_map(
        per_device,
        mesh=mesh,
        in_specs=placed,
        out_specs=(P("pix", None, None), P("pix", None, None), P("mem", "pix", None, None)),
        check_vma=False,
    )
```
